32 devices in a mesh: grp: 2 (over x), seq: 8 (over z, y), head: 2 (over core).
Axes of the slice: x: 2, y: 2, z: 4, core: 2. Of those that a mesh axis runs over, the one named last changes fastest.
Arguments:
- q_feat: bfloat16 [8192, 256], P(('grp', 'seq'), 'head'), parts along dimension 0, may hold values from -5 to 5
- k_feat: bfloat16 [8192, 256], P(('grp', 'seq'), 'head'), parts along dimension 0, may hold values from -5 to 5
- values: bfloat16 [8192, 2048], P(('grp', 'seq'), 'head'), parts along dimension 0, may hold values from -8 to 8
- win_query: bfloat16 [8192, 2048], P(('grp', 'seq'), 'head'), parts along dimension 0, may hold values from -20 to 20
- win_key: bfloat16 [8192, 2048], P(('grp', 'seq'), 'head'), parts along dimension 0, may hold values from -5 to 5
- log_gates: float32 [8192, 16], P(('grp', 'seq'), 'head'), parts along dimension 0, may hold values from -2.2 to 0
- conv_weight: float32 [3, 2048], P(None, 'head'), may hold values from -2.5 to 2.5
Outputs:
- mixed: bfloat16 [8192, 2048], P(('grp', 'seq'), 'head'), parts along dimension 0
The draws below stay inside these ranges and needn't reach their ends.
There are 2 independent parts, one for each index of `grp`. The reference program is written for one: setup_inputs(seed, part) draws one part's arguments, and reference() takes and returns one part's arrays. A program takes and returns all parts, laid end to end along the dimension named above; an argument that names none is the same for every part. Nothing has to cross between parts.
All inputs are finite; a program needn't handle non-finite values.
Results may differ from the reference program's by a relative error of at most 0.011.
Values may be sent and summed in bfloat16 or wider, within the bound.
A program may use at most 192 MiB of HBM per device.

```python
import math
import jax
import jax.numpy as jnp
from jax import lax

HEADS = 16
HEAD_DIM = 128
FEAT_DIM = 16
FEATURES = 273
WINDOW = 64
CONV = 3
BLOCK = 512
TOK_DEV = 512
DOCUMENT_TOKENS = 4096


def draw_win_key(key, part):
    shape = (DOCUMENT_TOKENS, HEADS * HEAD_DIM)
    drawn = jnp.clip(jax.random.normal(jax.random.fold_in(key, 11), shape, jnp.float32), -5.0, 5.0)
    return drawn.astype(jnp.bfloat16)


def draw_win_query(key, part):
    shape = (DOCUMENT_TOKENS, HEADS * HEAD_DIM)
    drawn = jnp.clip(jax.random.normal(jax.random.fold_in(key, 13), shape, jnp.float32), -5.0, 5.0)
    return drawn.astype(jnp.bfloat16)


def draw_k_feat(key, part):
    shape = (DOCUMENT_TOKENS, HEADS * FEAT_DIM)
    pieces = DOCUMENT_TOKENS // TOK_DEV
    phase = jax.random.randint(jax.random.fold_in(key, 41), (HEADS,), 0, 2)
    piece_index = jnp.arange(pieces)
    loud = (piece_index[:, None] + phase[None, :]) % 2 == 0
    level = jnp.where(loud, 2.5, 0.25).astype(jnp.float32)
    level = jnp.repeat(jnp.repeat(level, FEAT_DIM, axis=1), TOK_DEV, axis=0)
    noise = jax.random.normal(jax.random.fold_in(key, 42), shape, jnp.float32)
    return jnp.clip(noise * level, -5.0, 5.0).astype(jnp.bfloat16)


def draw_values(key, part):
    shape = (DOCUMENT_TOKENS, HEADS * HEAD_DIM)
    drawn = 2.0 * jax.random.normal(jax.random.fold_in(key, 21), shape, jnp.float32)
    return jnp.clip(drawn, -8.0, 8.0).astype(jnp.bfloat16)


def head_classes(key):
    order = jax.random.permutation(jax.random.fold_in(key, 31), HEADS)
    count = max(1, HEADS // 4)
    fast = order < count
    medium = (order >= count) & (order < 2 * count)
    return (fast, medium)


def draw_log_gates(key, part):
    fast, medium = head_classes(key)
    pieces = DOCUMENT_TOKENS // TOK_DEV
    slow_rate = jnp.exp(jax.random.uniform(jax.random.fold_in(key, 32), (HEADS,), jnp.float32, math.log(0.02), math.log(0.11))) / DOCUMENT_TOKENS
    fast_rate = 1.0 / jnp.exp(jax.random.uniform(jax.random.fold_in(key, 33), (HEADS,), jnp.float32, math.log(30.0), math.log(50.0)))
    medium_total = jnp.exp(jax.random.uniform(jax.random.fold_in(key, 38), (HEADS,), jnp.float32, math.log(4.65), math.log(5.0)))
    multiplier = jnp.exp(jax.random.uniform(jax.random.fold_in(key, 34), (pieces, HEADS), jnp.float32, -0.7, 0.7))
    medium_factor = jnp.exp(jax.random.uniform(jax.random.fold_in(key, 37), (pieces, HEADS), jnp.float32, 0.0, math.log(2.0)))
    drawn_rate = jnp.where(fast, fast_rate, slow_rate)[None, :] * multiplier
    medium_rate = medium_total[None, :] * medium_factor / TOK_DEV
    piece_rate = jnp.where(medium[None, :], medium_rate, drawn_rate)
    rates = jnp.repeat(piece_rate, TOK_DEV, axis=0)
    spike_location = jax.random.randint(jax.random.fold_in(key, 35), (3,), 0, DOCUMENT_TOKENS)
    spike_retained = jax.random.uniform(jax.random.fold_in(key, 36), (3,), jnp.float32, 0.5, 0.8)
    token_positions = jnp.arange(DOCUMENT_TOKENS)[:, None]
    spikes_list = jnp.sum(jnp.where(token_positions == spike_location[None, :], jnp.log(spike_retained)[None, :], 0.0), axis=1, keepdims=True)
    return (-rates + spikes_list).astype(jnp.float32)


def block_levels(key, dims, cuts, low, high):
    def one(dim, blocks):
        steps = jax.random.uniform(jax.random.fold_in(jax.random.fold_in(key, 6), dim), (blocks,), jnp.float32, low / len(cuts), high / len(cuts))
        return jnp.repeat(jnp.exp(steps), dims[dim] // blocks).reshape((-1,) + (1,) * (len(dims) - dim - 1))

    gain = one(*cuts[0])
    for cut in cuts[1:]:
        gain = gain * one(*cut)
    return gain


def normal_values(key, shape, scale, most, cuts=(), kind=jnp.bfloat16):
    entries = jax.random.normal(key, shape, jnp.float32) * scale
    if len(cuts) > 0:
        entries = block_levels(key, shape, cuts, -0.22, 0.18) * entries
    return jnp.clip(entries, min=-most, max=most).astype(kind)


def setup_inputs(seed: int = 0, part: int = 0) -> dict:
    seeds = jax.random.split(jax.random.key(seed), 8)
    part_splits = jax.random.split(jax.random.fold_in(seeds[7], part), 8)
    return {
        "q_feat": normal_values(part_splits[0], (DOCUMENT_TOKENS, HEADS * FEAT_DIM), 2.0, 5.0, ((0, 8), (1, 2))),
        "k_feat": draw_k_feat(jax.random.fold_in(jax.random.fold_in(seeds[7], part), 71), part),
        "values": draw_values(jax.random.fold_in(jax.random.fold_in(seeds[7], part), 71), part),
        "win_query": draw_win_query(jax.random.fold_in(jax.random.fold_in(seeds[7], part), 71), part),
        "win_key": draw_win_key(jax.random.fold_in(jax.random.fold_in(seeds[7], part), 71), part),
        "log_gates": draw_log_gates(jax.random.fold_in(jax.random.fold_in(seeds[7], part), 71), part),
        "conv_weight": normal_values(seeds[6], (CONV, HEADS * HEAD_DIM), 0.6, 2.5, ((1, 2),), jnp.float32),
    }


def taylor_map(features, heads):
    tok_rows = features.shape[0]
    width = features.shape[1] // heads
    spread = features.astype(jnp.float32).reshape(tok_rows, heads, width)
    linear = spread * width ** -0.25
    square = (spread[:, :, :, None] * spread[:, :, None, :]).reshape(tok_rows, heads, width * width) * (2.0 * width) ** -0.5
    ones = jnp.ones((tok_rows, heads, 1), jnp.float32)
    return jnp.concatenate([ones, linear, square], axis=2).astype(jnp.bfloat16)


def reference(q_feat, k_feat, values, win_query, win_key, log_gates, conv_weight):
    maximum_level = lax.Precision.HIGHEST
    count = DOCUMENT_TOKENS // BLOCK
    channels = HEADS * HEAD_DIM

    def split(array):
        return array.reshape((count, BLOCK) + array.shape[1:])

    block_inputs = (split(q_feat), split(k_feat), split(values), split(win_query), split(win_key), split(log_gates), jnp.arange(count, dtype=jnp.int32))
    start_carry = (jnp.zeros((HEADS, FEATURES, HEAD_DIM), jnp.float32), jnp.zeros((HEADS, FEATURES), jnp.float32),
                   jnp.zeros((WINDOW, channels), jnp.bfloat16), jnp.zeros((WINDOW, channels), jnp.bfloat16))
    causal = jnp.arange(BLOCK)[:, None] >= jnp.arange(BLOCK)[None, :]
    query_pos = jnp.arange(BLOCK)[:, None]
    key_pos = jnp.arange(BLOCK + WINDOW)[None, :] - WINDOW

    def advance(carry, inputs):
        running_state, norm_total, prev_key, prev_value = carry
        query_block, key_block, value_block, wq_block, wk_block, gate_block, index = inputs
        value_ext = jnp.concatenate([prev_value, value_block], axis=0)
        key_ext = jnp.concatenate([prev_key, wk_block], axis=0)
        convolved = jnp.zeros((BLOCK, channels), jnp.float32)
        for tap in range(CONV):
            convolved = convolved + conv_weight[tap][None, :] * value_ext[WINDOW - tap: WINDOW - tap + BLOCK].astype(jnp.float32)
        filtered_values = convolved.astype(jnp.bfloat16).reshape(BLOCK, HEADS, HEAD_DIM).astype(jnp.float32)
        query_features = taylor_map(query_block, HEADS).astype(jnp.float32)
        key_features = taylor_map(key_block, HEADS).astype(jnp.float32)
        cumulative = jnp.cumsum(gate_block, axis=0)
        cum_heads = cumulative.T
        decay_factor = jnp.exp(jnp.where(causal[None], cum_heads[:, :, None] - cum_heads[:, None, :], -jnp.inf))
        score_matrix = jnp.einsum("sjz,djz->jsd", query_features, key_features, precision=maximum_level) * decay_factor
        denominator = jnp.sum(score_matrix, axis=2).T
        numerator = jnp.einsum("hqk,khd->qhd", score_matrix.astype(jnp.bfloat16).astype(jnp.float32), filtered_values, precision=maximum_level)
        entering = jnp.exp(cumulative)
        numerator = numerator + entering[:, :, None] * jnp.einsum("qhf,hfd->qhd", query_features, running_state, precision=maximum_level)
        denominator = denominator + entering * jnp.einsum("qhf,hf->qh", query_features, norm_total, precision=maximum_level)
        linear = numerator / denominator[:, :, None]
        block_finish = cumulative[-1]
        retention = jnp.exp(block_finish[None, :] - cumulative)
        key_expanded = key_features * retention[:, :, None]
        running_state = jnp.exp(block_finish)[:, None, None] * running_state + jnp.einsum("mwv,mwr->wvr", key_expanded, filtered_values, precision=maximum_level)
        norm_total = jnp.exp(block_finish)[:, None] * norm_total + jnp.sum(key_expanded, axis=0)
        win_keys = key_ext.reshape(BLOCK + WINDOW, HEADS, HEAD_DIM).astype(jnp.float32)
        win_values = value_ext.reshape(BLOCK + WINDOW, HEADS, HEAD_DIM).astype(jnp.float32)
        win_queries = wq_block.reshape(BLOCK, HEADS, HEAD_DIM).astype(jnp.float32)
        win_scores = jnp.einsum("qhd,khd->hqk", win_queries, win_keys, precision=maximum_level) * HEAD_DIM ** -0.5
        valid = (key_pos <= query_pos) & (key_pos > query_pos - WINDOW) & (index * BLOCK + key_pos >= 0)
        win_scores = jnp.where(valid[None], win_scores, -jnp.inf)
        top = jnp.max(win_scores, axis=2, keepdims=True)
        weights = jnp.exp(win_scores - top)
        total = jnp.sum(weights, axis=2, keepdims=True)
        probs = (weights / total).astype(jnp.bfloat16).astype(jnp.float32)
        window_out = jnp.einsum("hqk,khd->qhd", probs, win_values, precision=maximum_level)
        mixed = (linear + window_out).astype(jnp.bfloat16).reshape(BLOCK, channels)
        return (running_state, norm_total, wk_block[BLOCK - WINDOW:], value_block[BLOCK - WINDOW:]), mixed

    final_carry, outputs = lax.scan(advance, start_carry, block_inputs)
    return outputs.reshape(DOCUMENT_TOKENS, channels)
```

```python
import functools

import jax
import jax.numpy as jnp
from jax import lax
from jax.experimental import pallas as pl
from jax.experimental.pallas import tpu as pltpu
from jax.sharding import PartitionSpec as P

WINDOW = 64
TILE = 128
FOLDED = 160
F32 = jnp.float32
BF16 = jnp.bfloat16
MESH = pl.DeviceIdType.MESH


def dot(a, b):
    return lax.dot_general(a, b, (((1,), (0,)), ((), ())), preferred_element_type=F32)


def dot_t(a, b):
    return lax.dot_general(a, b, (((1,), (1,)), ((), ())), preferred_element_type=F32)


def dot_first(a, b):
    return lax.dot_general(a, b, (((0,), (0,)), ((), ())), preferred_element_type=F32)


def fold_features(x, square_scale, pair_scale, linear_scale):
    rows = lax.broadcasted_iota(jnp.int32, x.shape, 0)
    scaled = x * pair_scale
    parts = [(x * square_scale) * x]
    for step in range(1, 8):
        parts.append(scaled * pltpu.roll(x, 16 - step, 0))
    half = scaled * pltpu.roll(x, 8, 0)
    parts.append(jnp.where(rows < 8, half, jnp.where(rows == 8, 1.0, 0.0)))
    parts.append(x * linear_scale)
    return jnp.concatenate([part.astype(BF16) for part in parts], axis=0)


def kernel(
    n, heads, size, width,
    qf, kf, gates, weight, values, win_key, win_query,
    out,
    vx, kx, wq, halo, vf, vw, qt, kt, phiq, numden, win, ccol, crow,
    s_send, s_recv, side, e_send, e_recv,
    in_sem, halo_send, halo_recv, ss_sem, sr_sem, ds_sem, dr_sem, es_sem, er_sem,
):
    me = lax.axis_index("seq")
    tok = qf.shape[0]
    per_head = n // heads
    rows = FOLDED // per_head
    tiles = tok // TILE
    tail = WINDOW

    load_v = pltpu.make_async_copy(values, vx.at[pl.ds(tail, tok)], in_sem.at[0])
    load_k = pltpu.make_async_copy(win_key, kx.at[pl.ds(tail, tok)], in_sem.at[1])
    load_q = pltpu.make_async_copy(win_query, wq, in_sem.at[2])
    load_v.start()
    load_k.start()
    load_q.start()

    barrier = pltpu.get_barrier_semaphore()
    for peer in range(n):
        @pl.when(peer != me)
        def _(peer=peer):
            pl.semaphore_signal(barrier, inc=1, device_id={"seq": peer}, device_id_type=MESH)

    @pl.when(me == 0)
    def _():
        vx[0:tail, :] = jnp.zeros((tail, heads * size), BF16)
        kx[0:tail, :] = jnp.zeros((tail, heads * size), BF16)
        halo[...] = jnp.zeros(halo.shape, BF16)

    pl.semaphore_wait(barrier, n - 1)

    nxt = lax.rem(me + 1, n)

    def halo_copies():
        short = pltpu.make_async_remote_copy(
            values.at[pl.ds(tok - 16, 16)], halo, halo_send.at[0], halo_recv.at[0],
            device_id={"seq": nxt}, device_id_type=MESH)
        long_v = pltpu.make_async_remote_copy(
            values.at[pl.ds(tok - tail, tail)], vx.at[pl.ds(0, tail)], halo_send.at[1], halo_recv.at[1],
            device_id={"seq": nxt}, device_id_type=MESH)
        long_k = pltpu.make_async_remote_copy(
            win_key.at[pl.ds(tok - tail, tail)], kx.at[pl.ds(0, tail)], halo_send.at[2], halo_recv.at[2],
            device_id={"seq": nxt}, device_id_type=MESH)
        return short, long_v, long_k

    @pl.when(me < n - 1)
    def _():
        for copy in halo_copies():
            copy.start()

    def s_copy(block):
        return pltpu.make_async_remote_copy(
            s_send.at[block], s_recv.at[me], ss_sem.at[block], sr_sem.at[me],
            device_id={"seq": block}, device_id_type=MESH)

    def s_arrival(source):
        return pltpu.make_async_remote_copy(
            s_send.at[source], s_recv.at[source], ss_sem.at[source], sr_sem.at[source],
            device_id={"seq": source}, device_id_type=MESH)

    def d_copy(peer):
        return pltpu.make_async_remote_copy(
            side.at[me], side.at[me], ds_sem.at[peer], dr_sem.at[me],
            device_id={"seq": peer}, device_id_type=MESH)

    def d_arrival(source):
        return pltpu.make_async_remote_copy(
            side.at[source], side.at[source], ds_sem.at[source], dr_sem.at[source],
            device_id={"seq": source}, device_id_type=MESH)

    def e_copy(peer):
        return pltpu.make_async_remote_copy(
            e_send.at[peer], e_recv.at[me], es_sem.at[peer], er_sem.at[me],
            device_id={"seq": peer}, device_id_type=MESH)

    def e_arrival(source):
        return pltpu.make_async_remote_copy(
            e_send.at[source], e_recv.at[source], es_sem.at[source], er_sem.at[source],
            device_id={"seq": source}, device_id_type=MESH)

    lower = jnp.where(
        lax.broadcasted_iota(jnp.int32, (tok, tok), 0) >= lax.broadcasted_iota(jnp.int32, (tok, tok), 1),
        1.0, 0.0).astype(BF16)
    wide = jnp.concatenate([gates[...], jnp.zeros((tok, 128 - heads), F32)], axis=1)
    upper = wide.astype(BF16)
    rest = wide - upper.astype(F32)
    middle = rest.astype(BF16)
    lowest = (rest - middle.astype(F32)).astype(BF16)
    total = dot(lower, upper) + (dot(lower, middle) + dot(lower, lowest))
    ccol[...] = total
    turned = total.T
    crow[...] = turned[0:heads, :]
    kt[...] = kf[...].astype(F32).T
    qt[...] = qf[...].astype(F32).T
    keep_row = jnp.exp(crow[:, tok - 1:tok] - crow[...])
    keep_hi = keep_row.astype(BF16)
    keep_lo = (keep_row - keep_hi.astype(F32)).astype(BF16)
    finish = jnp.exp(crow[:, tok - 1:tok])

    load_v.wait()

    @pl.when(me > 0)
    def _():
        halo_copies()[0].wait_recv()

    head_row = lax.broadcasted_iota(jnp.int32, (heads, FOLDED), 0)
    norm = jnp.zeros((heads, FOLDED), F32)
    for h in range(heads):
        lanes = slice(h * size, (h + 1) * size)
        phik = fold_features(kt[h * width:(h + 1) * width, :], 1.0, 1.0, 1.0)
        current = vx[tail:tail + tok, lanes].astype(F32)
        vf[8:8 + tok, :] = current
        vf[0:8, :] = halo[:, lanes].astype(F32)[8:16, :]
        conv = weight[0:1, lanes] * current
        for tap in range(1, weight.shape[0]):
            conv = conv + weight[tap:tap + 1, lanes] * vf[8 - tap:8 - tap + tok, :]
        conv = conv.astype(BF16)
        vw[h, :, 0:size] = conv
        vw[h, :, size:2 * size] = jnp.ones((tok, size), BF16)
        column = ccol[:, h:h + 1]
        keep = jnp.exp(ccol[tok - 1:tok, h:h + 1] - column)
        state = dot(phik, (conv.astype(F32) * keep).astype(BF16))
        norm_h = dot_t(keep_hi, phik) + dot_t(keep_lo, phik)
        norm = jnp.where(head_row == h, norm_h, norm)
        for b in range(per_head):
            block = h * per_head + b
            piece = state[b * rows:(b + 1) * rows, :].astype(BF16)

            @pl.when(block != me)
            def _(block=block, piece=piece):
                s_send[block] = piece
                s_copy(block).start()

            @pl.when(block == me)
            def _(piece=piece):
                s_recv[me] = piece

    side[me] = jnp.concatenate([norm, jnp.broadcast_to(finish, (heads, 256 - FOLDED))], axis=1)
    for peer in range(n):
        @pl.when(peer != me)
        def _(peer=peer):
            d_copy(peer).start()

    lane_head = lax.broadcasted_iota(jnp.int32, (tok, heads * width), 1) // width
    kt_narrow = kt[...].astype(BF16)
    q_quarter = qf[...] * jnp.asarray(0.25, BF16)
    diagonal = (lax.broadcasted_iota(jnp.int32, (TILE, TILE), 0)
                >= lax.broadcasted_iota(jnp.int32, (TILE, TILE), 1))
    for h in range(heads):
        lone = jnp.where(lane_head == h, q_quarter, jnp.zeros_like(q_quarter))
        for i in range(tiles):
            t0 = i * TILE
            reach = t0 + TILE
            x = dot(lone[t0:reach, :], kt_narrow[:, 0:reach])
            poly = 1.0 + x * (1.0 + 0.5 * x)
            gap = ccol[t0:reach, h:h + 1] - crow[h:h + 1, 0:reach]
            last = jnp.where(diagonal, gap[:, t0:reach], -1e30)
            if i > 0:
                gap = jnp.concatenate([gap[:, 0:t0], last], axis=1)
            else:
                gap = last
            score = (poly * jnp.exp(gap)).astype(BF16)
            numden[h, t0:reach, :] = dot(score, vw[h, 0:reach, :])

    for source in range(n):
        @pl.when(source != me)
        def _(source=source):
            s_arrival(source).wait_recv()
            d_arrival(source).wait_recv()

    mine = me // per_head
    running = jnp.zeros((rows, size), F32)
    for i in range(n):
        narrow = running.astype(BF16)

        @pl.when(i != me)
        def _(i=i, narrow=narrow):
            e_send[i] = narrow
            e_copy(i).start()

        @pl.when(i == me)
        def _(narrow=narrow):
            e_recv[me] = narrow

        fade = side[i, pl.ds(mine, 1), :][:, 192:193]
        running = fade * running + s_recv[i].astype(F32)

    norm_before = jnp.zeros((heads, 256), F32)
    for i in range(n):
        block = side[i]
        joined = block[:, 192:193] * norm_before + block
        norm_before = jnp.where(i < me, joined, norm_before)
    norm_col = jnp.concatenate([norm_before, jnp.zeros((128 - heads, 256), F32)], axis=0).T

    load_k.wait()
    load_q.wait()

    @pl.when(me > 0)
    def _():
        halo_copies()[1].wait_recv()
        halo_copies()[2].wait_recv()

    r = lax.broadcasted_iota(jnp.int32, (WINDOW, 2 * WINDOW), 0)
    j = lax.broadcasted_iota(jnp.int32, (WINDOW, 2 * WINDOW), 1)
    band = (j > r) & (j <= r + WINDOW)
    first = band & ((j >= WINDOW) | (me > 0))
    scale = size ** (-0.5)
    ones = jnp.ones((2 * WINDOW, size), BF16)
    for h in range(heads):
        lanes = slice(h * size, (h + 1) * size)
        for i in range(tok // WINDOW):
            t0 = i * WINDOW
            s = dot_t(wq[t0:t0 + WINDOW, lanes], kx[t0:t0 + 2 * WINDOW, lanes]) * scale
            s = jnp.where(first if i == 0 else band, s, -1e30)
            p = jnp.exp(s - jnp.max(s, axis=1, keepdims=True)).astype(BF16)
            pv = dot(p, jnp.concatenate([vx[t0:t0 + 2 * WINDOW, lanes], ones], axis=1))
            win[t0:t0 + WINDOW, lanes] = pv[:, 0:size] / pv[:, size:2 * size]

    for h in range(heads):
        phiq[h] = fold_features(qt[h * width:(h + 1) * width, :], 1.0 / 32, 1.0 / 16, 0.25)

    for source in range(n):
        @pl.when(source != me)
        def _(source=source):
            e_arrival(source).wait_recv()

    for h in range(heads):
        lanes = slice(h * size, (h + 1) * size)
        before = jnp.concatenate([e_recv[h * per_head + b] for b in range(per_head)], axis=0)
        norm_wide = jnp.broadcast_to(norm_col[0:FOLDED, h:h + 1], (FOLDED, size)).astype(BF16)
        both = dot_first(phiq[h], jnp.concatenate([before, norm_wide], axis=1))
        both = numden[h] + jnp.exp(ccol[:, h:h + 1]) * both
        out[:, lanes] = (both[:, 0:size] / both[:, size:2 * size] + win[:, lanes]).astype(BF16)

    @pl.when(me < n - 1)
    def _():
        for copy in halo_copies():
            copy.wait_send()

    for peer in range(n):
        @pl.when(peer != me)
        def _(peer=peer):
            s_copy(peer).wait_send()
            d_copy(peer).wait_send()
            e_copy(peer).wait_send()


def solution(mesh):
    n = mesh.shape["seq"]

    def local(q_feat, k_feat, values, win_query, win_key, log_gates, conv_weight):
        tok, channels = values.shape
        heads = log_gates.shape[1]
        size = channels // heads
        width = q_feat.shape[1] // heads
        rows = FOLDED * heads // n
        vmem = pl.BlockSpec(memory_space=pltpu.VMEM)
        anywhere = pl.BlockSpec(memory_space=pl.ANY)
        dma = pltpu.SemaphoreType.DMA
        return pl.pallas_call(
            functools.partial(kernel, n, heads, size, width),
            out_shape=jax.ShapeDtypeStruct((tok, channels), BF16),
            in_specs=[vmem] * 4 + [anywhere] * 3,
            out_specs=vmem,
            scratch_shapes=[
                pltpu.VMEM((tok + WINDOW, channels), BF16),
                pltpu.VMEM((tok + WINDOW, channels), BF16),
                pltpu.VMEM((tok, channels), BF16),
                pltpu.VMEM((16, channels), BF16),
                pltpu.VMEM((tok + 8, size), F32),
                pltpu.VMEM((heads, tok, 2 * size), BF16),
                pltpu.VMEM((heads * width, tok), F32),
                pltpu.VMEM((heads * width, tok), F32),
                pltpu.VMEM((heads, FOLDED, tok), BF16),
                pltpu.VMEM((heads, tok, 2 * size), F32),
                pltpu.VMEM((tok, channels), F32),
                pltpu.VMEM((tok, 128), F32),
                pltpu.VMEM((heads, tok), F32),
                pltpu.VMEM((n, rows, size), BF16),
                pltpu.VMEM((n, rows, size), BF16),
                pltpu.VMEM((n, heads, 256), F32),
                pltpu.VMEM((n, rows, size), BF16),
                pltpu.VMEM((n, rows, size), BF16),
                dma((3,)), dma((3,)), dma((3,)),
                dma((n,)), dma((n,)), dma((n,)), dma((n,)), dma((n,)), dma((n,)),
            ],
            compiler_params=pltpu.CompilerParams(
                collective_id=0, has_side_effects=True, vmem_limit_bytes=48 * 1024 * 1024),
        )(q_feat, k_feat, log_gates, conv_weight, values, win_key, win_query)

    shard = P(("grp", "seq"), "head")
    return jax.shard_map(
        local, mesh=mesh, in_specs=(shard,) * 6 + (P(None, "head"),), out_specs=shard, check_vma=False)
```

```python
import functools

import jax
import jax.numpy as jnp
from jax import lax
from jax.experimental import pallas as pl
from jax.experimental.pallas import tpu as pltpu
from jax.sharding import PartitionSpec as P

WINDOW = 64
TILE = 128
FOLDED = 160
F32 = jnp.float32
BF16 = jnp.bfloat16
MESH = pl.DeviceIdType.MESH


def dot(a, b):
    return lax.dot_general(a, b, (((1,), (0,)), ((), ())), preferred_element_type=F32)


def dot_t(a, b):
    return lax.dot_general(a, b, (((1,), (1,)), ((), ())), preferred_element_type=F32)


def dot_first(a, b):
    return lax.dot_general(a, b, (((0,), (0,)), ((), ())), preferred_element_type=F32)


def fold_features(x, square_scale, pair_scale, linear_scale):
    rows = lax.broadcasted_iota(jnp.int32, x.shape, 0)
    scaled = x * pair_scale
    parts = [(x * square_scale) * x]
    for step in range(1, 8):
        parts.append(scaled * pltpu.roll(x, 16 - step, 0))
    half = scaled * pltpu.roll(x, 8, 0)
    parts.append(jnp.where(rows < 8, half, jnp.where(rows == 8, 1.0, 0.0)))
    parts.append(x * linear_scale)
    return jnp.concatenate([part.astype(BF16) for part in parts], axis=0)


def kernel(
    n, heads, size, width,
    qf, kf, gates, weight, values, win_key, win_query,
    out,
    vx, kx, wq, halo, vf, vw, qt, kt, phiq, numden, win, ccol, crow,
    s_send, s_recv, side, e_send, e_recv,
    in_sem, halo_send, halo_recv, ss_sem, sr_sem, ds_sem, dr_sem, es_sem, er_sem,
):
    me = lax.axis_index("seq")
    tok = qf.shape[0]
    per_head = n // heads
    rows = FOLDED // per_head
    tiles = tok // TILE
    tail = WINDOW

    load_v = pltpu.make_async_copy(values, vx.at[pl.ds(tail, tok)], in_sem.at[0])
    load_k = pltpu.make_async_copy(win_key, kx.at[pl.ds(tail, tok)], in_sem.at[1])
    load_q = pltpu.make_async_copy(win_query, wq, in_sem.at[2])
    load_v.start()
    load_k.start()
    load_q.start()

    barrier = pltpu.get_barrier_semaphore()
    for peer in range(n):
        @pl.when(peer != me)
        def _(peer=peer):
            pl.semaphore_signal(barrier, inc=1, device_id={"seq": peer}, device_id_type=MESH)

    @pl.when(me == 0)
    def _():
        vx[0:tail, :] = jnp.zeros((tail, heads * size), BF16)
        kx[0:tail, :] = jnp.zeros((tail, heads * size), BF16)
        halo[...] = jnp.zeros(halo.shape, BF16)

    pl.semaphore_wait(barrier, n - 1)

    nxt = lax.rem(me + 1, n)

    def halo_copies():
        short = pltpu.make_async_remote_copy(
            values.at[pl.ds(tok - 16, 16)], halo, halo_send.at[0], halo_recv.at[0],
            device_id={"seq": nxt}, device_id_type=MESH)
        long_v = pltpu.make_async_remote_copy(
            values.at[pl.ds(tok - tail, tail)], vx.at[pl.ds(0, tail)], halo_send.at[1], halo_recv.at[1],
            device_id={"seq": nxt}, device_id_type=MESH)
        long_k = pltpu.make_async_remote_copy(
            win_key.at[pl.ds(tok - tail, tail)], kx.at[pl.ds(0, tail)], halo_send.at[2], halo_recv.at[2],
            device_id={"seq": nxt}, device_id_type=MESH)
        return short, long_v, long_k

    @pl.when(me < n - 1)
    def _():
        for copy in halo_copies():
            copy.start()

    def s_copy(block):
        return pltpu.make_async_remote_copy(
            s_send.at[block], s_recv.at[me], ss_sem.at[block], sr_sem.at[me],
            device_id={"seq": block}, device_id_type=MESH)

    def s_arrival(source):
        return pltpu.make_async_remote_copy(
            s_send.at[source], s_recv.at[source], ss_sem.at[source], sr_sem.at[source],
            device_id={"seq": source}, device_id_type=MESH)

    def d_copy(peer):
        return pltpu.make_async_remote_copy(
            side.at[me], side.at[me], ds_sem.at[peer], dr_sem.at[me],
            device_id={"seq": peer}, device_id_type=MESH)

    def d_arrival(source):
        return pltpu.make_async_remote_copy(
            side.at[source], side.at[source], ds_sem.at[source], dr_sem.at[source],
            device_id={"seq": source}, device_id_type=MESH)

    def e_copy(peer):
        return pltpu.make_async_remote_copy(
            e_send.at[peer], e_recv.at[me], es_sem.at[peer], er_sem.at[me],
            device_id={"seq": peer}, device_id_type=MESH)

    def e_arrival(source):
        return pltpu.make_async_remote_copy(
            e_send.at[source], e_recv.at[source], es_sem.at[source], er_sem.at[source],
            device_id={"seq": source}, device_id_type=MESH)

    before_or_at = jnp.where(
        lax.broadcasted_iota(jnp.int32, (tok, tok), 0) <= lax.broadcasted_iota(jnp.int32, (tok, tok), 1),
        1.0, 0.0).astype(BF16)
    upper = gates[...].astype(BF16)
    rest = gates[...] - upper.astype(F32)
    middle = rest.astype(BF16)
    lowest = (rest - middle.astype(F32)).astype(BF16)
    total = dot(jnp.concatenate([upper, middle, lowest], axis=0), before_or_at)
    total = total[0:heads] + (total[heads:2 * heads] + total[2 * heads:3 * heads])
    crow[...] = total
    ccol[...] = jnp.concatenate([total, jnp.zeros((128 - heads, tok), F32)], axis=0).T
    kt[...] = kf[...].astype(F32).T
    qt[...] = qf[...].astype(F32).T
    keep_row = jnp.exp(crow[:, tok - 1:tok] - crow[...])
    keep_hi = keep_row.astype(BF16)
    keep_lo = (keep_row - keep_hi.astype(F32)).astype(BF16)
    finish = jnp.exp(crow[:, tok - 1:tok])

    load_v.wait()

    @pl.when(me > 0)
    def _():
        halo_copies()[0].wait_recv()

    head_row = lax.broadcasted_iota(jnp.int32, (heads, FOLDED), 0)
    norm = jnp.zeros((heads, FOLDED), F32)
    for h in range(heads):
        lanes = slice(h * size, (h + 1) * size)
        phik = fold_features(kt[h * width:(h + 1) * width, :], 1.0, 1.0, 1.0)
        current = vx[tail:tail + tok, lanes].astype(F32)
        vf[8:8 + tok, lanes] = current
        vf[0:8, lanes] = halo[:, lanes].astype(F32)[8:16, :]
        conv = weight[0:1, lanes] * current
        for tap in range(1, weight.shape[0]):
            conv = conv + weight[tap:tap + 1, lanes] * vf[8 - tap:8 - tap + tok, lanes]
        conv = conv.astype(BF16)
        vw[h, :, 0:size] = conv
        vw[h, :, size:2 * size] = jnp.ones((tok, size), BF16)
        column = ccol[:, h:h + 1]
        keep = jnp.exp(ccol[tok - 1:tok, h:h + 1] - column)
        state = dot(phik, (conv.astype(F32) * keep).astype(BF16))
        norm_h = dot_t(keep_hi, phik) + dot_t(keep_lo, phik)
        norm = jnp.where(head_row == h, norm_h, norm)
        for b in range(per_head):
            block = h * per_head + b
            piece = state[b * rows:(b + 1) * rows, :].astype(BF16)

            @pl.when(block != me)
            def _(block=block, piece=piece):
                s_send[block] = piece
                s_copy(block).start()

            @pl.when(block == me)
            def _(piece=piece):
                s_recv[me] = piece

    side[me] = jnp.concatenate([norm, jnp.broadcast_to(finish, (heads, 256 - FOLDED))], axis=1)
    for peer in range(n):
        @pl.when(peer != me)
        def _(peer=peer):
            d_copy(peer).start()

    lane_head = lax.broadcasted_iota(jnp.int32, (tok, heads * width), 1) // width
    kt_narrow = kt[...].astype(BF16)
    q_quarter = qf[...] * jnp.asarray(0.25, BF16)
    diagonal = (lax.broadcasted_iota(jnp.int32, (TILE, TILE), 0)
                >= lax.broadcasted_iota(jnp.int32, (TILE, TILE), 1))
    for h in range(heads):
        lone = jnp.where(lane_head == h, q_quarter, jnp.zeros_like(q_quarter))
        for i in range(tiles):
            t0 = i * TILE
            reach = t0 + TILE
            x = dot(lone[t0:reach, :], kt_narrow[:, 0:reach])
            poly = 1.0 + x * (1.0 + 0.5 * x)
            gap = ccol[t0:reach, h:h + 1] - crow[h:h + 1, 0:reach]
            last = jnp.where(diagonal, gap[:, t0:reach], -1e30)
            if i > 0:
                gap = jnp.concatenate([gap[:, 0:t0], last], axis=1)
            else:
                gap = last
            score = (poly * jnp.exp(gap)).astype(BF16)
            numden[h, t0:reach, :] = dot(score, vw[h, 0:reach, :])

    for source in range(n):
        @pl.when(source != me)
        def _(source=source):
            s_arrival(source).wait_recv()
            d_arrival(source).wait_recv()

    mine = me // per_head
    running = jnp.zeros((rows, size), F32)
    for i in range(n):
        narrow = running.astype(BF16)

        @pl.when(i != me)
        def _(i=i, narrow=narrow):
            e_send[i] = narrow
            e_copy(i).start()

        @pl.when(i == me)
        def _(narrow=narrow):
            e_recv[me] = narrow

        fade = side[i, pl.ds(mine, 1), :][:, 192:193]
        running = fade * running + s_recv[i].astype(F32)

    norm_before = jnp.zeros((heads, 256), F32)
    for i in range(n):
        block = side[i]
        joined = block[:, 192:193] * norm_before + block
        norm_before = jnp.where(i < me, joined, norm_before)
    norm_col = jnp.concatenate([norm_before, jnp.zeros((128 - heads, 256), F32)], axis=0).T

    load_k.wait()
    load_q.wait()

    @pl.when(me > 0)
    def _():
        halo_copies()[1].wait_recv()
        halo_copies()[2].wait_recv()

    r = lax.broadcasted_iota(jnp.int32, (WINDOW, 2 * WINDOW), 0)
    j = lax.broadcasted_iota(jnp.int32, (WINDOW, 2 * WINDOW), 1)
    band = (j > r) & (j <= r + WINDOW)
    first = band & ((j >= WINDOW) | (me > 0))
    scale = size ** (-0.5)
    ones = jnp.ones((2 * WINDOW, size), BF16)
    for h in range(heads):
        lanes = slice(h * size, (h + 1) * size)
        for i in range(tok // WINDOW):
            t0 = i * WINDOW
            s = dot_t(wq[t0:t0 + WINDOW, lanes], kx[t0:t0 + 2 * WINDOW, lanes]) * scale
            s = jnp.where(first if i == 0 else band, s, -1e30)
            p = jnp.exp(s - jnp.max(s, axis=1, keepdims=True)).astype(BF16)
            pv = dot(p, jnp.concatenate([vx[t0:t0 + 2 * WINDOW, lanes], ones], axis=1))
            win[t0:t0 + WINDOW, lanes] = pv[:, 0:size] / pv[:, size:2 * size]

    for h in range(heads):
        phiq[h] = fold_features(qt[h * width:(h + 1) * width, :], 1.0 / 32, 1.0 / 16, 0.25)

    for source in range(n):
        @pl.when(source != me)
        def _(source=source):
            e_arrival(source).wait_recv()

    for h in range(heads):
        lanes = slice(h * size, (h + 1) * size)
        before = jnp.concatenate([e_recv[h * per_head + b] for b in range(per_head)], axis=0)
        norm_wide = jnp.broadcast_to(norm_col[0:FOLDED, h:h + 1], (FOLDED, size)).astype(BF16)
        both = dot_first(phiq[h], jnp.concatenate([before, norm_wide], axis=1))
        both = numden[h] + jnp.exp(ccol[:, h:h + 1]) * both
        out[:, lanes] = (both[:, 0:size] / both[:, size:2 * size] + win[:, lanes]).astype(BF16)

    @pl.when(me < n - 1)
    def _():
        for copy in halo_copies():
            copy.wait_send()

    for peer in range(n):
        @pl.when(peer != me)
        def _(peer=peer):
            s_copy(peer).wait_send()
            d_copy(peer).wait_send()
            e_copy(peer).wait_send()


def solution(mesh):
    n = mesh.shape["seq"]

    def local(q_feat, k_feat, values, win_query, win_key, log_gates, conv_weight):
        tok, channels = values.shape
        heads = log_gates.shape[1]
        size = channels // heads
        width = q_feat.shape[1] // heads
        rows = FOLDED * heads // n
        vmem = pl.BlockSpec(memory_space=pltpu.VMEM)
        anywhere = pl.BlockSpec(memory_space=pltpu.HBM)
        dma = pltpu.SemaphoreType.DMA
        return pl.pallas_call(
            functools.partial(kernel, n, heads, size, width),
            out_shape=jax.ShapeDtypeStruct((tok, channels), BF16),
            in_specs=[vmem] * 4 + [anywhere] * 3,
            out_specs=vmem,
            scratch_shapes=[
                pltpu.VMEM((tok + WINDOW, channels), BF16),
                pltpu.VMEM((tok + WINDOW, channels), BF16),
                pltpu.VMEM((tok, channels), BF16),
                pltpu.VMEM((16, channels), BF16),
                pltpu.VMEM((tok + 8, channels), F32),
                pltpu.VMEM((heads, tok, 2 * size), BF16),
                pltpu.VMEM((heads * width, tok), F32),
                pltpu.VMEM((heads * width, tok), F32),
                pltpu.VMEM((heads, FOLDED, tok), BF16),
                pltpu.VMEM((heads, tok, 2 * size), F32),
                pltpu.VMEM((tok, channels), F32),
                pltpu.VMEM((tok, 128), F32),
                pltpu.VMEM((heads, tok), F32),
                pltpu.VMEM((n, rows, size), BF16),
                pltpu.VMEM((n, rows, size), BF16),
                pltpu.VMEM((n, heads, 256), F32),
                pltpu.VMEM((n, rows, size), BF16),
                pltpu.VMEM((n, rows, size), BF16),
                dma((3,)), dma((3,)), dma((3,)),
                dma((n,)), dma((n,)), dma((n,)), dma((n,)), dma((n,)), dma((n,)),
            ],
            compiler_params=pltpu.CompilerParams(
                collective_id=0, has_side_effects=True, vmem_limit_bytes=56 * 1024 * 1024),
        )(q_feat, k_feat, log_gates.T, conv_weight, values, win_key, win_query)

    shard = P(("grp", "seq"), "head")
    return jax.shard_map(
        local, mesh=mesh, in_specs=(shard,) * 6 + (P(None, "head"),), out_specs=shard, check_vma=False)
```

```python
import functools

import jax
import jax.numpy as jnp
from jax import lax
from jax.experimental import pallas as pl
from jax.experimental.pallas import tpu as pltpu
from jax.sharding import PartitionSpec as P

WINDOW = 64
TILE = 128
FOLDED = 160
F32 = jnp.float32
BF16 = jnp.bfloat16
MESH = pl.DeviceIdType.MESH


def dot(a, b):
    return lax.dot_general(a, b, (((1,), (0,)), ((), ())), preferred_element_type=F32)


def dot_t(a, b):
    return lax.dot_general(a, b, (((1,), (1,)), ((), ())), preferred_element_type=F32)


def dot_first(a, b):
    return lax.dot_general(a, b, (((0,), (0,)), ((), ())), preferred_element_type=F32)


def fold_features(x, square_scale, pair_scale, linear_scale):
    rows = lax.broadcasted_iota(jnp.int32, x.shape, 0)
    scaled = x * pair_scale
    parts = [(x * square_scale) * x]
    for step in range(1, 8):
        parts.append(scaled * pltpu.roll(x, 16 - step, 0))
    half = scaled * pltpu.roll(x, 8, 0)
    parts.append(jnp.where(rows < 8, half, jnp.where(rows == 8, 1.0, 0.0)))
    parts.append(x * linear_scale)
    return jnp.concatenate([part.astype(BF16) for part in parts], axis=0)


def kernel(
    n, heads, size, width,
    qf, kf, gates, weight, values, win_key, win_query,
    out,
    vx, kx, wq, halo, vf, vw, qt, kt, phik, phiq, numden, win, ccol, crow,
    s_send, s_recv, side, e_send, e_recv,
    in_sem, halo_send, halo_recv, ss_sem, sr_sem, ds_sem, dr_sem, es_sem, er_sem,
):
    me = lax.axis_index("seq")
    tok = qf.shape[0]
    per_head = n // heads
    rows = FOLDED // per_head
    tiles = tok // TILE
    tail = WINDOW

    load_v = pltpu.make_async_copy(values, vx.at[pl.ds(tail, tok)], in_sem.at[0])
    load_k = pltpu.make_async_copy(win_key, kx.at[pl.ds(tail, tok)], in_sem.at[1])
    load_q = pltpu.make_async_copy(win_query, wq, in_sem.at[2])
    load_v.start()
    load_k.start()
    load_q.start()

    barrier = pltpu.get_barrier_semaphore()
    for peer in range(n):
        @pl.when(peer != me)
        def _(peer=peer):
            pl.semaphore_signal(barrier, inc=1, device_id={"seq": peer}, device_id_type=MESH)

    @pl.when(me == 0)
    def _():
        vx[0:tail, :] = jnp.zeros((tail, heads * size), BF16)
        kx[0:tail, :] = jnp.zeros((tail, heads * size), BF16)
        halo[...] = jnp.zeros(halo.shape, BF16)

    nxt = lax.rem(me + 1, n)

    def halo_copies():
        short = pltpu.make_async_remote_copy(
            values.at[pl.ds(tok - 16, 16)], halo, halo_send.at[0], halo_recv.at[0],
            device_id={"seq": nxt}, device_id_type=MESH)
        long_v = pltpu.make_async_remote_copy(
            values.at[pl.ds(tok - tail, tail)], vx.at[pl.ds(0, tail)], halo_send.at[1], halo_recv.at[1],
            device_id={"seq": nxt}, device_id_type=MESH)
        long_k = pltpu.make_async_remote_copy(
            win_key.at[pl.ds(tok - tail, tail)], kx.at[pl.ds(0, tail)], halo_send.at[2], halo_recv.at[2],
            device_id={"seq": nxt}, device_id_type=MESH)
        return short, long_v, long_k

    def s_copy(block):
        return pltpu.make_async_remote_copy(
            s_send.at[block], s_recv.at[me], ss_sem.at[block], sr_sem.at[me],
            device_id={"seq": block}, device_id_type=MESH)

    def s_arrival(source):
        return pltpu.make_async_remote_copy(
            s_send.at[source], s_recv.at[source], ss_sem.at[source], sr_sem.at[source],
            device_id={"seq": source}, device_id_type=MESH)

    def d_copy(peer):
        return pltpu.make_async_remote_copy(
            side.at[me], side.at[me], ds_sem.at[peer], dr_sem.at[me],
            device_id={"seq": peer}, device_id_type=MESH)

    def d_arrival(source):
        return pltpu.make_async_remote_copy(
            side.at[source], side.at[source], ds_sem.at[source], dr_sem.at[source],
            device_id={"seq": source}, device_id_type=MESH)

    def e_copy(peer):
        return pltpu.make_async_remote_copy(
            e_send.at[peer], e_recv.at[me], es_sem.at[peer], er_sem.at[me],
            device_id={"seq": peer}, device_id_type=MESH)

    def e_arrival(source):
        return pltpu.make_async_remote_copy(
            e_send.at[source], e_recv.at[source], es_sem.at[source], er_sem.at[source],
            device_id={"seq": source}, device_id_type=MESH)

    before_or_at = jnp.where(
        lax.broadcasted_iota(jnp.int32, (tok, tok), 0) <= lax.broadcasted_iota(jnp.int32, (tok, tok), 1),
        1.0, 0.0).astype(BF16)
    upper = gates[...].astype(BF16)
    rest = gates[...] - upper.astype(F32)
    middle = rest.astype(BF16)
    lowest = (rest - middle.astype(F32)).astype(BF16)
    total = dot(jnp.concatenate([upper, middle, lowest], axis=0), before_or_at)
    total = total[0:heads] + (total[heads:2 * heads] + total[2 * heads:3 * heads])
    crow[...] = total
    ccol[...] = jnp.concatenate([total, jnp.zeros((128 - heads, tok), F32)], axis=0).T
    kt[...] = kf[...].astype(F32).T
    qt[...] = qf[...].astype(F32).T
    keep_row = jnp.exp(crow[:, tok - 1:tok] - crow[...])
    keep_hi = keep_row.astype(BF16)
    keep_lo = (keep_row - keep_hi.astype(F32)).astype(BF16)
    finish = jnp.exp(crow[:, tok - 1:tok])

    pl.semaphore_wait(barrier, n - 1)

    @pl.when(me < n - 1)
    def _():
        for copy in halo_copies():
            copy.start()

    for h in range(heads):
        phik[h] = fold_features(kt[h * width:(h + 1) * width, :], 1.0, 1.0, 1.0)
    load_v.wait()

    @pl.when(me > 0)
    def _():
        halo_copies()[0].wait_recv()

    head_row = lax.broadcasted_iota(jnp.int32, (heads, FOLDED), 0)
    norm = jnp.zeros((heads, FOLDED), F32)
    for h in range(heads):
        lanes = slice(h * size, (h + 1) * size)
        current = vx[tail:tail + tok, lanes].astype(F32)
        vf[8:8 + tok, lanes] = current
        vf[0:8, lanes] = halo[:, lanes].astype(F32)[8:16, :]
        conv = weight[0:1, lanes] * current
        for tap in range(1, weight.shape[0]):
            conv = conv + weight[tap:tap + 1, lanes] * vf[8 - tap:8 - tap + tok, lanes]
        conv = conv.astype(BF16)
        vw[h, :, 0:size] = conv
        vw[h, :, size:2 * size] = jnp.ones((tok, size), BF16)
        column = ccol[:, h:h + 1]
        keep = jnp.exp(ccol[tok - 1:tok, h:h + 1] - column)
        state = dot(phik[h], (conv.astype(F32) * keep).astype(BF16))
        norm_h = dot_t(keep_hi, phik[h]) + dot_t(keep_lo, phik[h])
        norm = jnp.where(head_row == h, norm_h, norm)
        for b in range(per_head):
            block = h * per_head + b
            s_send[block] = state[b * rows:(b + 1) * rows, :].astype(BF16)

    s_recv[me] = s_send[me]
    side[me] = jnp.concatenate([norm, jnp.broadcast_to(finish, (heads, 256 - FOLDED))], axis=1)

    @pl.when(me < n - 1)
    def _():
        for offset in range(1, n):
            peer = lax.rem(me + offset, n)
            s_copy(peer).start()
            d_copy(peer).start()

    lane_head = lax.broadcasted_iota(jnp.int32, (tok, heads * width), 1) // width
    kt_narrow = kt[...].astype(BF16)
    q_quarter = qf[...] * jnp.asarray(0.25, BF16)
    diagonal = (lax.broadcasted_iota(jnp.int32, (TILE, TILE), 0)
                >= lax.broadcasted_iota(jnp.int32, (TILE, TILE), 1))
    for h in range(heads):
        lone = jnp.where(lane_head == h, q_quarter, jnp.zeros_like(q_quarter))
        for i in range(tiles):
            t0 = i * TILE
            reach = t0 + TILE
            x = dot(lone[t0:reach, :], kt_narrow[:, 0:reach])
            poly = 1.0 + x * (1.0 + 0.5 * x)
            gap = ccol[t0:reach, h:h + 1] - crow[h:h + 1, 0:reach]
            last = jnp.where(diagonal, gap[:, t0:reach], -1e30)
            if i > 0:
                gap = jnp.concatenate([gap[:, 0:t0], last], axis=1)
            else:
                gap = last
            score = (poly * jnp.exp(gap)).astype(BF16)
            numden[h, t0:reach, :] = dot(score, vw[h, 0:reach, :])

    load_k.wait()
    load_q.wait()

    @pl.when(me > 0)
    def _():
        halo_copies()[1].wait_recv()
        halo_copies()[2].wait_recv()

    r = lax.broadcasted_iota(jnp.int32, (WINDOW, 2 * WINDOW), 0)
    j = lax.broadcasted_iota(jnp.int32, (WINDOW, 2 * WINDOW), 1)
    band = (j > r) & (j <= r + WINDOW)
    steps = tok // WINDOW
    bias = jnp.where(band, 0.0, -1e30)
    bias = jnp.concatenate(
        [jnp.where(band & ((j >= WINDOW) | (me > 0)), 0.0, -1e30)] + [bias] * (steps - 1), axis=0)
    scale = size ** (-0.5)
    ones = jnp.ones((2 * WINDOW, size), BF16)

    def slide(h):
        lanes = slice(h * size, (h + 1) * size)
        s = jnp.concatenate([
            dot_t(wq[i * WINDOW:(i + 1) * WINDOW, lanes], kx[i * WINDOW:(i + 2) * WINDOW, lanes])
            for i in range(steps)], axis=0)
        s = s * scale + bias
        p = jnp.exp(s - jnp.max(s, axis=1, keepdims=True)).astype(BF16)
        pv = jnp.concatenate([
            dot(p[i * WINDOW:(i + 1) * WINDOW, :],
                jnp.concatenate([vx[i * WINDOW:(i + 2) * WINDOW, lanes], ones], axis=1))
            for i in range(steps)], axis=0)
        win[:, lanes] = pv[:, 0:size] / pv[:, size:2 * size]

    for h in range(heads // 2):
        slide(h)

    for source in range(n - 1):
        @pl.when(source != me)
        def _(source=source):
            s_arrival(source).wait_recv()
            d_arrival(source).wait_recv()

    mine = me // per_head
    running = jnp.zeros((rows, size), F32)
    e_send[0] = running.astype(BF16)
    for i in range(n - 1):
        fade = side[i, pl.ds(mine, 1), :][:, 192:193]
        running = fade * running + s_recv[i].astype(F32)
        e_send[i + 1] = running.astype(BF16)

    e_recv[me] = e_send[me]
    for offset in range(1, n):
        peer = lax.rem(me + offset, n)

        @pl.when(peer > 0)
        def _(peer=peer):
            e_copy(peer).start()

    @pl.when(me == 0)
    def _():
        e_recv[...] = jnp.zeros(e_recv.shape, BF16)

    norm_before = jnp.zeros((heads, 256), F32)
    for i in range(n - 1):
        block = side[i]
        joined = block[:, 192:193] * norm_before + block
        norm_before = jnp.where(i < me, joined, norm_before)
    norm_col = jnp.concatenate([norm_before, jnp.zeros((128 - heads, 256), F32)], axis=0).T

    for h in range(heads // 2, heads):
        slide(h)

    for h in range(heads):
        phiq[h] = fold_features(qt[h * width:(h + 1) * width, :], 1.0 / 32, 1.0 / 16, 0.25)

    for source in range(n):
        @pl.when((source != me) & (me > 0))
        def _(source=source):
            e_arrival(source).wait_recv()

    for h in range(heads):
        lanes = slice(h * size, (h + 1) * size)
        before = jnp.concatenate([e_recv[h * per_head + b] for b in range(per_head)], axis=0)
        norm_wide = jnp.broadcast_to(norm_col[0:FOLDED, h:h + 1], (FOLDED, size)).astype(BF16)
        both = dot_first(phiq[h], jnp.concatenate([before, norm_wide], axis=1))
        both = numden[h] + jnp.exp(ccol[:, h:h + 1]) * both
        out[:, lanes] = (both[:, 0:size] / both[:, size:2 * size] + win[:, lanes]).astype(BF16)

    @pl.when(me < n - 1)
    def _():
        for copy in halo_copies():
            copy.wait_send()

    for peer in range(n):
        @pl.when((peer != me) & (me < n - 1))
        def _(peer=peer):
            s_copy(peer).wait_send()
            d_copy(peer).wait_send()

        if peer > 0:
            @pl.when(peer != me)
            def _(peer=peer):
                e_copy(peer).wait_send()


def solution(mesh):
    n = mesh.shape["seq"]

    def local(q_feat, k_feat, values, win_query, win_key, log_gates, conv_weight):
        tok, channels = values.shape
        heads = log_gates.shape[1]
        size = channels // heads
        width = q_feat.shape[1] // heads
        rows = FOLDED * heads // n
        vmem = pl.BlockSpec(memory_space=pltpu.VMEM)
        anywhere = pl.BlockSpec(memory_space=pltpu.HBM)
        dma = pltpu.SemaphoreType.DMA
        return pl.pallas_call(
            functools.partial(kernel, n, heads, size, width),
            out_shape=jax.ShapeDtypeStruct((tok, channels), BF16),
            in_specs=[vmem] * 4 + [anywhere] * 3,
            out_specs=vmem,
            scratch_shapes=[
                pltpu.VMEM((tok + WINDOW, channels), BF16),
                pltpu.VMEM((tok + WINDOW, channels), BF16),
                pltpu.VMEM((tok, channels), BF16),
                pltpu.VMEM((16, channels), BF16),
                pltpu.VMEM((tok + 8, channels), F32),
                pltpu.VMEM((heads, tok, 2 * size), BF16),
                pltpu.VMEM((heads * width, tok), F32),
                pltpu.VMEM((heads * width, tok), F32),
                pltpu.VMEM((heads, FOLDED, tok), BF16),
                pltpu.VMEM((heads, FOLDED, tok), BF16),
                pltpu.VMEM((heads, tok, 2 * size), F32),
                pltpu.VMEM((tok, channels), F32),
                pltpu.VMEM((tok, 128), F32),
                pltpu.VMEM((heads, tok), F32),
                pltpu.VMEM((n, rows, size), BF16),
                pltpu.VMEM((n, rows, size), BF16),
                pltpu.VMEM((n, heads, 256), F32),
                pltpu.VMEM((n, rows, size), BF16),
                pltpu.VMEM((n, rows, size), BF16),
                dma((3,)), dma((3,)), dma((3,)),
                dma((n,)), dma((n,)), dma((n,)), dma((n,)), dma((n,)), dma((n,)),
            ],
            compiler_params=pltpu.CompilerParams(
                collective_id=0, has_side_effects=True, vmem_limit_bytes=32 * 1024 * 1024),
        )(q_feat, k_feat, log_gates.T, conv_weight, values, win_key, win_query)

    shard = P(("grp", "seq"), "head")
    return jax.shard_map(
        local, mesh=mesh, in_specs=(shard,) * 6 + (P(None, "head"),), out_specs=shard, check_vma=False)
```

```python
import functools

import jax
import jax.numpy as jnp
from jax import lax
from jax.experimental import pallas as pl
from jax.experimental.pallas import tpu as pltpu
from jax.sharding import PartitionSpec as P

WINDOW = 64
TILE = 128
FOLDED = 160
F32 = jnp.float32
BF16 = jnp.bfloat16
MESH = pl.DeviceIdType.MESH


def dot(a, b):
    return lax.dot_general(a, b, (((1,), (0,)), ((), ())), preferred_element_type=F32)


def dot_t(a, b):
    return lax.dot_general(a, b, (((1,), (1,)), ((), ())), preferred_element_type=F32)


def dot_first(a, b):
    return lax.dot_general(a, b, (((0,), (0,)), ((), ())), preferred_element_type=F32)


def fold_features(x, square_scale, pair_scale, linear_scale):
    rows = lax.broadcasted_iota(jnp.int32, x.shape, 0)
    scaled = x * pair_scale
    parts = [(x * square_scale) * x]
    for step in range(1, 8):
        parts.append(scaled * pltpu.roll(x, 16 - step, 0))
    half = scaled * pltpu.roll(x, 8, 0)
    parts.append(jnp.where(rows < 8, half, jnp.where(rows == 8, 1.0, 0.0)))
    parts.append(x * linear_scale)
    return jnp.concatenate([part.astype(BF16) for part in parts], axis=0)


def kernel(
    n, heads, size, width,
    qf, kf, gates, weight, values, win_key, win_query,
    out,
    vx, kx, wq, halo, vf, vw, qt, kt, phik, phiq, numden, win, ccol, crow,
    s_send, s_recv, side, e_send, e_recv,
    in_sem, halo_send, halo_recv, ss_sem, sr_sem, ds_sem, dr_sem, es_sem, er_sem,
):
    me = lax.axis_index("seq")
    tok = qf.shape[0]
    per_head = n // heads
    rows = FOLDED // per_head
    tiles = tok // TILE
    tail = WINDOW

    load_v = pltpu.make_async_copy(values, vx.at[pl.ds(tail, tok)], in_sem.at[0])
    load_k = pltpu.make_async_copy(win_key, kx.at[pl.ds(tail, tok)], in_sem.at[1])
    load_q = pltpu.make_async_copy(win_query, wq, in_sem.at[2])
    load_v.start()
    load_k.start()
    load_q.start()

    barrier = pltpu.get_barrier_semaphore()
    for peer in range(n):
        @pl.when(peer != me)
        def _(peer=peer):
            pl.semaphore_signal(barrier, inc=1, device_id={"seq": peer}, device_id_type=MESH)

    @pl.when(me == 0)
    def _():
        vx[0:tail, :] = jnp.zeros((tail, heads * size), BF16)
        kx[0:tail, :] = jnp.zeros((tail, heads * size), BF16)
        halo[...] = jnp.zeros(halo.shape, BF16)

    nxt = lax.rem(me + 1, n)

    def halo_copies():
        short = pltpu.make_async_remote_copy(
            values.at[pl.ds(tok - 16, 16)], halo, halo_send.at[0], halo_recv.at[0],
            device_id={"seq": nxt}, device_id_type=MESH)
        long_v = pltpu.make_async_remote_copy(
            values.at[pl.ds(tok - tail, tail)], vx.at[pl.ds(0, tail)], halo_send.at[1], halo_recv.at[1],
            device_id={"seq": nxt}, device_id_type=MESH)
        long_k = pltpu.make_async_remote_copy(
            win_key.at[pl.ds(tok - tail, tail)], kx.at[pl.ds(0, tail)], halo_send.at[2], halo_recv.at[2],
            device_id={"seq": nxt}, device_id_type=MESH)
        return short, long_v, long_k

    def s_copy(block):
        return pltpu.make_async_remote_copy(
            s_send.at[block], s_recv.at[me], ss_sem.at[block], sr_sem.at[me],
            device_id={"seq": block}, device_id_type=MESH)

    def s_arrival(source):
        return pltpu.make_async_remote_copy(
            s_send.at[source], s_recv.at[source], ss_sem.at[source], sr_sem.at[source],
            device_id={"seq": source}, device_id_type=MESH)

    def d_copy(peer):
        return pltpu.make_async_remote_copy(
            side.at[me], side.at[me], ds_sem.at[peer], dr_sem.at[me],
            device_id={"seq": peer}, device_id_type=MESH)

    def d_arrival(source):
        return pltpu.make_async_remote_copy(
            side.at[source], side.at[source], ds_sem.at[source], dr_sem.at[source],
            device_id={"seq": source}, device_id_type=MESH)

    def e_copy(peer):
        return pltpu.make_async_remote_copy(
            e_send.at[peer], e_recv.at[me], es_sem.at[peer], er_sem.at[me],
            device_id={"seq": peer}, device_id_type=MESH)

    def e_arrival(source):
        return pltpu.make_async_remote_copy(
            e_send.at[source], e_recv.at[source], es_sem.at[source], er_sem.at[source],
            device_id={"seq": source}, device_id_type=MESH)

    before_or_at = jnp.where(
        lax.broadcasted_iota(jnp.int32, (tok, tok), 0) <= lax.broadcasted_iota(jnp.int32, (tok, tok), 1),
        1.0, 0.0).astype(BF16)
    upper = gates[...].astype(BF16)
    rest = gates[...] - upper.astype(F32)
    middle = rest.astype(BF16)
    lowest = (rest - middle.astype(F32)).astype(BF16)
    total = dot(jnp.concatenate([upper, middle, lowest], axis=0), before_or_at)
    total = total[0:heads] + (total[heads:2 * heads] + total[2 * heads:3 * heads])
    crow[...] = total
    ccol[...] = jnp.concatenate([total, jnp.zeros((128 - heads, tok), F32)], axis=0).T
    kt[...] = kf[...].astype(F32).T
    qt[...] = qf[...].astype(F32).T
    keep_row = jnp.exp(crow[:, tok - 1:tok] - crow[...])
    keep_hi = keep_row.astype(BF16)
    keep_lo = (keep_row - keep_hi.astype(F32)).astype(BF16)
    finish = jnp.exp(crow[:, tok - 1:tok])

    pl.semaphore_wait(barrier, n - 1)

    @pl.when(me < n - 1)
    def _():
        for copy in halo_copies():
            copy.start()

    for h in range(heads):
        phik[h] = fold_features(kt[h * width:(h + 1) * width, :], 1.0, 1.0, 1.0)
    load_v.wait()

    @pl.when(me > 0)
    def _():
        halo_copies()[0].wait_recv()

    head_row = lax.broadcasted_iota(jnp.int32, (heads, FOLDED), 0)
    norm = jnp.zeros((heads, FOLDED), F32)
    for h in range(heads):
        lanes = slice(h * size, (h + 1) * size)
        current = vx[tail:tail + tok, lanes].astype(F32)
        vf[8:8 + tok, lanes] = current
        vf[0:8, lanes] = halo[:, lanes].astype(F32)[8:16, :]
        conv = weight[0:1, lanes] * current
        for tap in range(1, weight.shape[0]):
            conv = conv + weight[tap:tap + 1, lanes] * vf[8 - tap:8 - tap + tok, lanes]
        conv = conv.astype(BF16)
        vw[h, :, 0:size] = conv
        vw[h, :, size:2 * size] = jnp.ones((tok, size), BF16)
        column = ccol[:, h:h + 1]
        keep = jnp.exp(ccol[tok - 1:tok, h:h + 1] - column)
        state = dot(phik[h], (conv.astype(F32) * keep).astype(BF16))
        norm_h = dot_t(keep_hi, phik[h]) + dot_t(keep_lo, phik[h])
        norm = jnp.where(head_row == h, norm_h, norm)
        for b in range(per_head):
            block = h * per_head + b
            s_send[block] = state[b * rows:(b + 1) * rows, :].astype(BF16)

    s_recv[me] = s_send[me]
    side[me] = jnp.concatenate([norm, jnp.broadcast_to(finish, (heads, 256 - FOLDED))], axis=1)

    @pl.when(me < n - 1)
    def _():
        for offset in range(1, n):
            peer = lax.rem(me + offset, n)
            s_copy(peer).start()
            d_copy(peer).start()

    lane_head = lax.broadcasted_iota(jnp.int32, (tok, heads * width), 1) // width
    kt_narrow = kt[...].astype(BF16)
    q_quarter = qf[...] * jnp.asarray(0.25, BF16)
    diagonal = (lax.broadcasted_iota(jnp.int32, (TILE, TILE), 0)
                >= lax.broadcasted_iota(jnp.int32, (TILE, TILE), 1))
    for h in range(heads):
        lone = jnp.where(lane_head == h, q_quarter, jnp.zeros_like(q_quarter))
        for i in range(tiles):
            t0 = i * TILE
            reach = t0 + TILE
            x = dot(lone[t0:reach, :], kt_narrow[:, 0:reach])
            poly = 1.0 + x * (1.0 + 0.5 * x)
            gap = ccol[t0:reach, h:h + 1] - crow[h:h + 1, 0:reach]
            last = jnp.where(diagonal, gap[:, t0:reach], -1e30)
            if i > 0:
                gap = jnp.concatenate([gap[:, 0:t0], last], axis=1)
            else:
                gap = last
            score = (poly * jnp.exp(gap)).astype(BF16)
            numden[h, t0:reach, :] = dot(score, vw[h, 0:reach, :])

    load_k.wait()
    load_q.wait()

    @pl.when(me > 0)
    def _():
        halo_copies()[1].wait_recv()
        halo_copies()[2].wait_recv()

    r = lax.broadcasted_iota(jnp.int32, (WINDOW, 2 * WINDOW), 0)
    j = lax.broadcasted_iota(jnp.int32, (WINDOW, 2 * WINDOW), 1)
    band = (j > r) & (j <= r + WINDOW)
    steps = tok // WINDOW
    bias = jnp.where(band, 0.0, -1e30)
    bias = jnp.concatenate(
        [jnp.where(band & ((j >= WINDOW) | (me > 0)), 0.0, -1e30)] + [bias] * (steps - 1), axis=0)
    scale = size ** (-0.5)
    ones = jnp.ones((2 * WINDOW, size), BF16)

    def slide(h):
        lanes = slice(h * size, (h + 1) * size)
        s = jnp.concatenate([
            dot_t(wq[i * WINDOW:(i + 1) * WINDOW, lanes], kx[i * WINDOW:(i + 2) * WINDOW, lanes])
            for i in range(steps)], axis=0)
        s = s * scale + bias
        p = jnp.exp(s - jnp.max(s, axis=1, keepdims=True)).astype(BF16)
        pv = jnp.concatenate([
            dot(p[i * WINDOW:(i + 1) * WINDOW, :],
                jnp.concatenate([vx[i * WINDOW:(i + 2) * WINDOW, lanes], ones], axis=1))
            for i in range(steps)], axis=0)
        win[:, lanes] = pv[:, 0:size] / pv[:, size:2 * size]

    for h in range(heads // 2):
        slide(h)

    for source in range(n - 1):
        @pl.when(source != me)
        def _(source=source):
            s_arrival(source).wait_recv()
            d_arrival(source).wait_recv()

    mine = me // per_head
    running = jnp.zeros((rows, size), F32)
    e_send[0] = running.astype(BF16)
    for i in range(n - 1):
        fade = side[i, pl.ds(mine, 1), :][:, 192:193]
        running = fade * running + s_recv[i].astype(F32)
        e_send[i + 1] = running.astype(BF16)

    e_recv[me] = e_send[me]
    for offset in range(1, n):
        peer = lax.rem(me + offset, n)

        @pl.when(peer > 0)
        def _(peer=peer):
            e_copy(peer).start()

    @pl.when(me == 0)
    def _():
        e_recv[...] = jnp.zeros(e_recv.shape, BF16)

    norm_before = jnp.zeros((heads, 256), F32)
    for i in range(n - 1):
        block = side[i]
        joined = block[:, 192:193] * norm_before + block
        norm_before = jnp.where(i < me, joined, norm_before)
    norm_col = jnp.concatenate([norm_before, jnp.zeros((128 - heads, 256), F32)], axis=0).T

    for h in range(heads // 2, heads):
        slide(h)

    for h in range(heads):
        phiq[h] = fold_features(qt[h * width:(h + 1) * width, :], 1.0 / 32, 1.0 / 16, 0.25)

    for source in range(n):
        @pl.when((source != me) & (me > 0))
        def _(source=source):
            e_arrival(source).wait_recv()

    for h in range(heads):
        lanes = slice(h * size, (h + 1) * size)
        before = jnp.concatenate([e_recv[h * per_head + b] for b in range(per_head)], axis=0)
        norm_wide = jnp.broadcast_to(norm_col[0:FOLDED, h:h + 1], (FOLDED, size)).astype(BF16)
        both = dot_first(phiq[h], jnp.concatenate([before, norm_wide], axis=1))
        both = numden[h] + jnp.exp(ccol[:, h:h + 1]) * both
        out[:, lanes] = (both[:, 0:size] / both[:, size:2 * size] + win[:, lanes]).astype(BF16)

    @pl.when(me < n - 1)
    def _():
        for copy in halo_copies():
            copy.wait_send()

    for peer in range(n):
        @pl.when((peer != me) & (me < n - 1))
        def _(peer=peer):
            s_copy(peer).wait_send()
            d_copy(peer).wait_send()

        if peer > 0:
            @pl.when(peer != me)
            def _(peer=peer):
                e_copy(peer).wait_send()


def solution(mesh):
    n = mesh.shape["seq"]

    def local(q_feat, k_feat, values, win_query, win_key, log_gates, conv_weight):
        tok, channels = values.shape
        heads = log_gates.shape[1]
        size = channels // heads
        width = q_feat.shape[1] // heads
        rows = FOLDED * heads // n
        vmem = pl.BlockSpec(memory_space=pltpu.VMEM)
        anywhere = pl.BlockSpec(memory_space=pltpu.HBM)
        dma = pltpu.SemaphoreType.DMA
        return pl.pallas_call(
            functools.partial(kernel, n, heads, size, width),
            out_shape=jax.ShapeDtypeStruct((tok, channels), BF16),
            in_specs=[vmem] * 4 + [anywhere] * 3,
            out_specs=vmem,
            scratch_shapes=[
                pltpu.VMEM((tok + WINDOW, channels), BF16),
                pltpu.VMEM((tok + WINDOW, channels), BF16),
                pltpu.VMEM((tok, channels), BF16),
                pltpu.VMEM((16, channels), BF16),
                pltpu.VMEM((tok + 8, channels), F32),
                pltpu.VMEM((heads, tok, 2 * size), BF16),
                pltpu.VMEM((heads * width, tok), F32),
                pltpu.VMEM((heads * width, tok), F32),
                pltpu.VMEM((heads, FOLDED, tok), BF16),
                pltpu.VMEM((heads, FOLDED, tok), BF16),
                pltpu.VMEM((heads, tok, 2 * size), F32),
                pltpu.VMEM((tok, channels), F32),
                pltpu.VMEM((tok, 128), F32),
                pltpu.VMEM((heads, tok), F32),
                pltpu.VMEM((n, rows, size), BF16),
                pltpu.VMEM((n, rows, size), BF16),
                pltpu.VMEM((n, heads, 256), F32),
                pltpu.VMEM((n, rows, size), BF16),
                pltpu.VMEM((n, rows, size), BF16),
                dma((3,)), dma((3,)), dma((3,)),
                dma((n,)), dma((n,)), dma((n,)), dma((n,)), dma((n,)), dma((n,)),
            ],
            compiler_params=pltpu.CompilerParams(
                collective_id=0, has_side_effects=True, vmem_limit_bytes=54 * 1024 * 1024),
        )(q_feat, k_feat, log_gates.T, conv_weight, values, win_key, win_query)

    shard = P(("grp", "seq"), "head")
    return jax.shard_map(
        local, mesh=mesh, in_specs=(shard,) * 6 + (P(None, "head"),), out_specs=shard, check_vma=False)
```

```python
import functools

import jax
import jax.numpy as jnp
from jax import lax
from jax.experimental import pallas as pl
from jax.experimental.pallas import tpu as pltpu
from jax.sharding import PartitionSpec as P

WINDOW = 64
TILE = 128
FOLDED = 160
F32 = jnp.float32
BF16 = jnp.bfloat16
MESH = pl.DeviceIdType.MESH


def dot(a, b):
    return lax.dot_general(a, b, (((1,), (0,)), ((), ())), preferred_element_type=F32)


def dot_t(a, b):
    return lax.dot_general(a, b, (((1,), (1,)), ((), ())), preferred_element_type=F32)


def dot_first(a, b):
    return lax.dot_general(a, b, (((0,), (0,)), ((), ())), preferred_element_type=F32)


def fold_features(x, square_scale, pair_scale, linear_scale):
    rows = lax.broadcasted_iota(jnp.int32, x.shape, 0)
    scaled = x * pair_scale
    parts = [(x * square_scale) * x]
    for step in range(1, 8):
        parts.append(scaled * pltpu.roll(x, 16 - step, 0))
    half = scaled * pltpu.roll(x, 8, 0)
    parts.append(jnp.where(rows < 8, half, jnp.where(rows == 8, 1.0, 0.0)))
    parts.append(x * linear_scale)
    return jnp.concatenate([part.astype(BF16) for part in parts], axis=0)


def kernel(
    n, heads, size, width,
    qf, kf, gates, weight, values, win_key, win_query,
    out,
    vx, kx, wq, halo, vf, vw, qt, kt, phik, phiq, numden, win, ccol, crow,
    s_send, s_recv, side, e_send, e_recv,
    in_sem, halo_send, halo_recv, ss_sem, sr_sem, ds_sem, dr_sem, es_sem, er_sem,
):
    me = lax.axis_index("seq")
    tok = qf.shape[0]
    per_head = n // heads
    rows = FOLDED // per_head
    tiles = tok // TILE
    tail = WINDOW

    load_v = pltpu.make_async_copy(values, vx.at[pl.ds(tail, tok)], in_sem.at[0])
    load_k = pltpu.make_async_copy(win_key, kx.at[pl.ds(tail, tok)], in_sem.at[1])
    load_q = pltpu.make_async_copy(win_query, wq, in_sem.at[2])
    load_v.start()
    load_k.start()
    load_q.start()

    barrier = pltpu.get_barrier_semaphore()
    for peer in range(n):
        @pl.when(peer != me)
        def _(peer=peer):
            pl.semaphore_signal(barrier, inc=1, device_id={"seq": peer}, device_id_type=MESH)

    @pl.when(me == 0)
    def _():
        vx[0:tail, :] = jnp.zeros((tail, heads * size), BF16)
        kx[0:tail, :] = jnp.zeros((tail, heads * size), BF16)
        halo[...] = jnp.zeros(halo.shape, BF16)

    nxt = lax.rem(me + 1, n)

    def halo_copies():
        short = pltpu.make_async_remote_copy(
            values.at[pl.ds(tok - 16, 16)], halo, halo_send.at[0], halo_recv.at[0],
            device_id={"seq": nxt}, device_id_type=MESH)
        long_v = pltpu.make_async_remote_copy(
            values.at[pl.ds(tok - tail, tail)], vx.at[pl.ds(0, tail)], halo_send.at[1], halo_recv.at[1],
            device_id={"seq": nxt}, device_id_type=MESH)
        long_k = pltpu.make_async_remote_copy(
            win_key.at[pl.ds(tok - tail, tail)], kx.at[pl.ds(0, tail)], halo_send.at[2], halo_recv.at[2],
            device_id={"seq": nxt}, device_id_type=MESH)
        return short, long_v, long_k

    def s_copy(block):
        return pltpu.make_async_remote_copy(
            s_send.at[block], s_recv.at[me], ss_sem.at[block], sr_sem.at[me],
            device_id={"seq": block}, device_id_type=MESH)

    def s_arrival(source):
        return pltpu.make_async_remote_copy(
            s_send.at[source], s_recv.at[source], ss_sem.at[source], sr_sem.at[source],
            device_id={"seq": source}, device_id_type=MESH)

    def d_copy(peer):
        return pltpu.make_async_remote_copy(
            side.at[me], side.at[me], ds_sem.at[peer], dr_sem.at[me],
            device_id={"seq": peer}, device_id_type=MESH)

    def d_arrival(source):
        return pltpu.make_async_remote_copy(
            side.at[source], side.at[source], ds_sem.at[source], dr_sem.at[source],
            device_id={"seq": source}, device_id_type=MESH)

    def e_copy(peer):
        return pltpu.make_async_remote_copy(
            e_send.at[peer], e_recv.at[me], es_sem.at[peer], er_sem.at[me],
            device_id={"seq": peer}, device_id_type=MESH)

    def e_arrival(source):
        return pltpu.make_async_remote_copy(
            e_send.at[source], e_recv.at[source], es_sem.at[source], er_sem.at[source],
            device_id={"seq": source}, device_id_type=MESH)

    before_or_at = jnp.where(
        lax.broadcasted_iota(jnp.int32, (tok, tok), 0) <= lax.broadcasted_iota(jnp.int32, (tok, tok), 1),
        1.0, 0.0).astype(BF16)
    upper = gates[...].astype(BF16)
    rest = gates[...] - upper.astype(F32)
    middle = rest.astype(BF16)
    lowest = (rest - middle.astype(F32)).astype(BF16)
    total = dot(jnp.concatenate([upper, middle, lowest], axis=0), before_or_at)
    total = total[0:heads] + (total[heads:2 * heads] + total[2 * heads:3 * heads])
    crow[...] = total
    ccol[...] = jnp.concatenate([total, jnp.zeros((128 - heads, tok), F32)], axis=0).T
    kt[...] = kf[...].astype(F32).T
    qt[...] = qf[...].astype(F32).T
    keep_row = jnp.exp(crow[:, tok - 1:tok] - crow[...])
    keep_hi = keep_row.astype(BF16)
    keep_lo = (keep_row - keep_hi.astype(F32)).astype(BF16)
    finish = jnp.exp(crow[:, tok - 1:tok])

    pl.semaphore_wait(barrier, n - 1)

    @pl.when(me < n - 1)
    def _():
        for copy in halo_copies():
            copy.start()

    for h in range(heads):
        phik[h] = fold_features(kt[h * width:(h + 1) * width, :], 1.0, 1.0, 1.0)
    load_v.wait()

    @pl.when(me > 0)
    def _():
        halo_copies()[0].wait_recv()

    head_row = lax.broadcasted_iota(jnp.int32, (heads, FOLDED), 0)
    norm = jnp.zeros((heads, FOLDED), F32)
    for h in range(heads):
        lanes = slice(h * size, (h + 1) * size)
        current = vx[tail:tail + tok, lanes].astype(F32)
        vf[8:8 + tok, lanes] = current
        vf[0:8, lanes] = halo[:, lanes].astype(F32)[8:16, :]
        conv = weight[0:1, lanes] * current
        for tap in range(1, weight.shape[0]):
            conv = conv + weight[tap:tap + 1, lanes] * vf[8 - tap:8 - tap + tok, lanes]
        conv = conv.astype(BF16)
        vw[h, :, 0:size] = conv
        vw[h, :, size:2 * size] = jnp.ones((tok, size), BF16)
        column = ccol[:, h:h + 1]
        keep = jnp.exp(ccol[tok - 1:tok, h:h + 1] - column)
        state = dot(phik[h], (conv.astype(F32) * keep).astype(BF16))
        norm_h = dot_t(keep_hi, phik[h]) + dot_t(keep_lo, phik[h])
        norm = jnp.where(head_row == h, norm_h, norm)
        for b in range(per_head):
            block = h * per_head + b
            s_send[block] = state[b * rows:(b + 1) * rows, :].astype(BF16)
        if h + 1 in (heads // 2, heads):
            half = n // 2
            start = 0 if h + 1 == heads // 2 else half
            for turn in range(half):
                peer = start + lax.rem(me + turn, half)

                @pl.when((peer != me) & (me < n - 1))
                def _(peer=peer):
                    s_copy(peer).start()

    side[me] = jnp.concatenate([norm, jnp.broadcast_to(finish, (heads, 256 - FOLDED))], axis=1)

    @pl.when(me < n - 1)
    def _():
        for offset in range(1, n):
            d_copy(lax.rem(me + offset, n)).start()

    s_recv[me] = s_send[me]

    lane_head = lax.broadcasted_iota(jnp.int32, (tok, heads * width), 1) // width
    kt_narrow = kt[...].astype(BF16)
    q_quarter = qf[...] * jnp.asarray(0.25, BF16)
    diagonal = (lax.broadcasted_iota(jnp.int32, (TILE, TILE), 0)
                >= lax.broadcasted_iota(jnp.int32, (TILE, TILE), 1))
    for h in range(heads):
        lone = jnp.where(lane_head == h, q_quarter, jnp.zeros_like(q_quarter))
        for i in range(tiles):
            t0 = i * TILE
            reach = t0 + TILE
            x = dot(lone[t0:reach, :], kt_narrow[:, 0:reach])
            poly = 1.0 + x * (1.0 + 0.5 * x)
            gap = ccol[t0:reach, h:h + 1] - crow[h:h + 1, 0:reach]
            last = jnp.where(diagonal, gap[:, t0:reach], -1e30)
            if i > 0:
                gap = jnp.concatenate([gap[:, 0:t0], last], axis=1)
            else:
                gap = last
            score = (poly * jnp.exp(gap)).astype(BF16)
            numden[h, t0:reach, :] = dot(score, vw[h, 0:reach, :])

    load_k.wait()
    load_q.wait()

    @pl.when(me > 0)
    def _():
        halo_copies()[1].wait_recv()
        halo_copies()[2].wait_recv()

    r = lax.broadcasted_iota(jnp.int32, (WINDOW, 2 * WINDOW), 0)
    j = lax.broadcasted_iota(jnp.int32, (WINDOW, 2 * WINDOW), 1)
    band = (j > r) & (j <= r + WINDOW)
    steps = tok // WINDOW
    bias = jnp.where(band, 0.0, -1e30)
    bias = jnp.concatenate(
        [jnp.where(band & ((j >= WINDOW) | (me > 0)), 0.0, -1e30)] + [bias] * (steps - 1), axis=0)
    scale = size ** (-0.5)
    ones = jnp.ones((2 * WINDOW, size), BF16)

    def slide(h):
        lanes = slice(h * size, (h + 1) * size)
        s = jnp.concatenate([
            dot_t(wq[i * WINDOW:(i + 1) * WINDOW, lanes], kx[i * WINDOW:(i + 2) * WINDOW, lanes])
            for i in range(steps)], axis=0)
        s = s * scale + bias
        p = jnp.exp(s - jnp.max(s, axis=1, keepdims=True)).astype(BF16)
        pv = jnp.concatenate([
            dot(p[i * WINDOW:(i + 1) * WINDOW, :],
                jnp.concatenate([vx[i * WINDOW:(i + 2) * WINDOW, lanes], ones], axis=1))
            for i in range(steps)], axis=0)
        win[:, lanes] = pv[:, 0:size] / pv[:, size:2 * size]

    for h in range(heads // 2):
        slide(h)

    for source in range(n - 1):
        @pl.when(source != me)
        def _(source=source):
            s_arrival(source).wait_recv()
            d_arrival(source).wait_recv()

    mine = me // per_head
    running = jnp.zeros((rows, size), F32)
    e_send[0] = running.astype(BF16)
    for i in range(n - 1):
        fade = side[i, pl.ds(mine, 1), :][:, 192:193]
        running = fade * running + s_recv[i].astype(F32)
        e_send[i + 1] = running.astype(BF16)

    e_recv[me] = e_send[me]
    for offset in range(1, n):
        peer = lax.rem(me + offset, n)

        @pl.when(peer > 0)
        def _(peer=peer):
            e_copy(peer).start()

    @pl.when(me == 0)
    def _():
        e_recv[...] = jnp.zeros(e_recv.shape, BF16)

    norm_before = jnp.zeros((heads, 256), F32)
    for i in range(n - 1):
        block = side[i]
        joined = block[:, 192:193] * norm_before + block
        norm_before = jnp.where(i < me, joined, norm_before)
    norm_col = jnp.concatenate([norm_before, jnp.zeros((128 - heads, 256), F32)], axis=0).T

    for h in range(heads // 2, heads):
        slide(h)

    for h in range(heads):
        phiq[h] = fold_features(qt[h * width:(h + 1) * width, :], 1.0 / 32, 1.0 / 16, 0.25)

    for source in range(n):
        @pl.when((source != me) & (me > 0))
        def _(source=source):
            e_arrival(source).wait_recv()

    for h in range(heads):
        lanes = slice(h * size, (h + 1) * size)
        before = jnp.concatenate([e_recv[h * per_head + b] for b in range(per_head)], axis=0)
        norm_wide = jnp.broadcast_to(norm_col[0:FOLDED, h:h + 1], (FOLDED, size)).astype(BF16)
        both = dot_first(phiq[h], jnp.concatenate([before, norm_wide], axis=1))
        both = numden[h] + jnp.exp(ccol[:, h:h + 1]) * both
        out[:, lanes] = (both[:, 0:size] / both[:, size:2 * size] + win[:, lanes]).astype(BF16)

    @pl.when(me < n - 1)
    def _():
        for copy in halo_copies():
            copy.wait_send()

    for peer in range(n):
        @pl.when((peer != me) & (me < n - 1))
        def _(peer=peer):
            s_copy(peer).wait_send()
            d_copy(peer).wait_send()

        if peer > 0:
            @pl.when(peer != me)
            def _(peer=peer):
                e_copy(peer).wait_send()


def solution(mesh):
    n = mesh.shape["seq"]

    def local(q_feat, k_feat, values, win_query, win_key, log_gates, conv_weight):
        tok, channels = values.shape
        heads = log_gates.shape[1]
        size = channels // heads
        width = q_feat.shape[1] // heads
        rows = FOLDED * heads // n
        vmem = pl.BlockSpec(memory_space=pltpu.VMEM)
        anywhere = pl.BlockSpec(memory_space=pltpu.HBM)
        dma = pltpu.SemaphoreType.DMA
        return pl.pallas_call(
            functools.partial(kernel, n, heads, size, width),
            out_shape=jax.ShapeDtypeStruct((tok, channels), BF16),
            in_specs=[vmem] * 4 + [anywhere] * 3,
            out_specs=vmem,
            scratch_shapes=[
                pltpu.VMEM((tok + WINDOW, channels), BF16),
                pltpu.VMEM((tok + WINDOW, channels), BF16),
                pltpu.VMEM((tok, channels), BF16),
                pltpu.VMEM((16, channels), BF16),
                pltpu.VMEM((tok + 8, channels), F32),
                pltpu.VMEM((heads, tok, 2 * size), BF16),
                pltpu.VMEM((heads * width, tok), F32),
                pltpu.VMEM((heads * width, tok), F32),
                pltpu.VMEM((heads, FOLDED, tok), BF16),
                pltpu.VMEM((heads, FOLDED, tok), BF16),
                pltpu.VMEM((heads, tok, 2 * size), F32),
                pltpu.VMEM((tok, channels), F32),
                pltpu.VMEM((tok, 128), F32),
                pltpu.VMEM((heads, tok), F32),
                pltpu.VMEM((n, rows, size), BF16),
                pltpu.VMEM((n, rows, size), BF16),
                pltpu.VMEM((n, heads, 256), F32),
                pltpu.VMEM((n, rows, size), BF16),
                pltpu.VMEM((n, rows, size), BF16),
                dma((3,)), dma((3,)), dma((3,)),
                dma((n,)), dma((n,)), dma((n,)), dma((n,)), dma((n,)), dma((n,)),
            ],
            compiler_params=pltpu.CompilerParams(
                collective_id=0, has_side_effects=True, vmem_limit_bytes=54 * 1024 * 1024),
        )(q_feat, k_feat, log_gates.T, conv_weight, values, win_key, win_query)

    shard = P(("grp", "seq"), "head")
    return jax.shard_map(
        local, mesh=mesh, in_specs=(shard,) * 6 + (P(None, "head"),), out_specs=shard, check_vma=False)
```
